128 devices in a mesh: row: 8 (over x, z_hi), col: 16 (over y, z_lo, core).
Axes of the slice: x: 4, y: 4, z: 4 (z_hi: 2, z_lo: 2; z = z_hi * 2 + z_lo), core: 2. Of those that a mesh axis runs over, the one named last changes fastest.
Arguments:
- matrix: float32 [16384, 16384], P('row', 'col'), may hold values from -6 to 6
- factor_inverse: float32 [512, 512], replicated, may hold values from -0.25 to 0.25
- panel: int32 [1], replicated, may hold values from 0 to 31
- split_index: int32 [1], replicated, may hold values from 4096 to 12288
Outputs:
- halves: float32 [16384, 512], P('col')
The draws below stay inside these ranges and needn't reach their ends.
All inputs are finite; a program needn't handle non-finite values.
Results may differ from the reference program's by a relative error of at most 0.000071.
Values sent between devices are 32-bit elements; how exact they have to be, the bound alone decides.
No kernel may reach another device: no remote copies, remote signals or barrier semaphores. Data moves between devices by JAX's collectives and lax.ppermute only.
A program may use at most 64 MiB of HBM per device.

```python
import jax
import jax.numpy as jnp
from jax import lax

N = 16384
B = 512


def levels(key, extent, cuts, low, high):
    factor_of = 1.0
    for dim, parts in cuts:
        draws = jax.random.uniform(jax.random.fold_in(jax.random.fold_in(key, 6), dim), (parts,), jnp.float32, low / len(cuts), high / len(cuts))
        factor_of = factor_of * jnp.repeat(jnp.exp(draws), extent[dim] // parts).reshape((-1,) + (1,) * (len(extent) - 1 - dim))
    return factor_of


def gaussian(own_key, shape, width, limit, split=(), kind=jnp.bfloat16):
    gain = levels(own_key, shape, split, -0.22, 0.18) if split else 1.0
    drawn = jax.random.normal(own_key, shape, jnp.float32) * width * gain
    return jnp.minimum(jnp.maximum(drawn, -limit), limit).astype(kind)


def setup_inputs(seed: int = 0) -> dict:
    key_of = jax.random.split(jax.random.key(seed), 5)
    matrix = gaussian(key_of[0], (N, N), 1.0, 6.0, ((0, 8), (1, 16)), jnp.float32)
    factor_inverse = gaussian(key_of[1], (B, B), B ** -0.5, 0.25, (), jnp.float32)
    panel = jax.random.randint(key_of[2], (1,), 0, N // B).astype(jnp.int32)
    split_index = jax.random.randint(key_of[3], (1,), N // 4, 3 * N // 4 + 1).astype(jnp.int32)
    return dict(matrix=matrix, factor_inverse=factor_inverse, panel=panel, split_index=split_index)


def reference(matrix, factor_inverse, panel, split_index):
    start = panel[0] * B
    ident = (jnp.arange(N, dtype=jnp.int32)[:, None] == start + jnp.arange(B, dtype=jnp.int32)[None, :]).astype(jnp.float32)
    columns = lax.dynamic_slice_in_dim(matrix, start.astype(jnp.int32), B, 1)
    gram = lax.dot_general(matrix, columns, (((0,), (0,)), ((), ())), precision=lax.Precision.HIGHEST, preferred_element_type=jnp.float32) / N + ident
    factor = lax.dot_general(gram, factor_inverse, (((1,), (1,)), ((), ())), precision=lax.Precision.HIGHEST, preferred_element_type=jnp.float32)
    projector = 0.5 * (ident + jnp.dot(matrix, factor, precision=lax.Precision.HIGHEST, preferred_element_type=jnp.float32))
    index = jnp.arange(N, dtype=jnp.int32)
    keep = (index < N // 2) == (index < split_index[0])
    return jnp.where(keep[:, None], projector, jnp.float32(0.0))
```

```python
import jax
import jax.numpy as jnp
from jax import lax
from jax.sharding import Mesh, PartitionSpec as P

ROW = ("x", "zh")
GRID = ("y", "zl")
ALL = ("x", "zh", "y", "zl", "core")
SIZES = (4, 2, 4, 2, 2)
HIGH = lax.Precision.HIGH
BLK = 128


def dot(a, b, dims, precision=HIGH):
    return lax.dot_general(a, b, (dims, ((), ())), precision=precision, preferred_element_type=jnp.float32)


def offsets(d1, d2):
    return [(i * 2 + j, (i + d1) % 4 * 2 + (j + d2) % 2) for i in range(4) for j in range(2)]


OFFS = [(2, 1), (2, 0), (1, 1), (3, 1), (1, 0), (3, 0), (0, 1)]


def gather_blocks(block, axes, mine):
    rows = block.shape[0]
    out = jnp.zeros((8 * rows, block.shape[1]), block.dtype)
    out = lax.dynamic_update_slice_in_dim(out, block, mine * rows, 0)
    a, b = mine // 2, mine % 2
    for d1, d2 in OFFS:
        got = lax.ppermute(block, axes, offsets(d1, d2))
        src = (a - d1) % 4 * 2 + (b - d2) % 2
        out = lax.dynamic_update_slice_in_dim(out, got, src * rows, 0)
    return out


def turn_map():
    g = {0: 2, 1: 3, 3: 1, 2: 0}
    return lambda x, y: (x + g[(y - x) % 4]) % 4


def turn_perm():
    f = turn_map()
    perm = []
    for x in range(4):
        for zh in range(2):
            for y in range(4):
                for zl in range(2):
                    for c in range(2):
                        src = (((x * 2 + zh) * 4 + y) * 2 + zl) * 2 + c
                        dst = (((f(x, y) * 2 + zl) * 4 + x) * 2 + zh) * 2 + c
                        perm.append((src, dst))
    return perm


def per_device(matrix, factor_inverse, panel, split_index):
    rows_loc, cols_loc = matrix.shape
    width = factor_inverse.shape[0]
    x, zh = lax.axis_index("x"), lax.axis_index("zh")
    y, zl, core = lax.axis_index("y"), lax.axis_index("zl"), lax.axis_index("core")
    row = x * 2 + zh
    chip = y * 2 + zl
    col = chip * 2 + core
    order = cols_loc * 16
    half = rows_loc // 2
    start = panel[0] * width
    owner = start // cols_loc
    offset = start - owner * cols_loc
    swap = [(0, 1), (1, 0)]

    piece = lax.dynamic_slice_in_dim(matrix, offset, width, 1)
    give = lax.dynamic_slice_in_dim(piece, (1 - core) * half, half, 0)
    keep = lax.dynamic_slice_in_dim(piece, core * half, half, 0)
    got = lax.ppermute(give, "core", swap)
    mine = jnp.where(owner % 2 == core, keep, got)
    parts = lax.all_to_all(mine, GRID, 0, 0, tiled=True)
    block = lax.dynamic_slice_in_dim(parts, owner // 2 * BLK, BLK, 0)
    own_half = gather_blocks(block, GRID, chip)
    other_half = lax.ppermute(own_half, "core", swap)
    upper = jnp.where(core == 0, own_half, other_half)
    lower = jnp.where(core == 0, other_half, own_half)
    columns = jnp.concatenate([upper, lower], 0)

    partial = dot(matrix, columns, ((0,), (0,)))
    parts = lax.all_to_all(partial, ROW, 0, 0, tiled=True).reshape(8, BLK, width)
    rows_global = col * cols_loc + row * BLK + jnp.arange(BLK, dtype=jnp.int32)
    diag = (rows_global[:, None] == start + jnp.arange(width, dtype=jnp.int32)[None, :]).astype(jnp.float32)
    gram = jnp.sum(parts, 0) / order + diag
    fblock = dot(gram, factor_inverse, ((1,), (1,)), lax.Precision.HIGHEST)
    factor = gather_blocks(fblock, ROW, row)

    product = dot(matrix, factor, ((1,), (0,)))
    give = lax.dynamic_slice_in_dim(product, (1 - core) * half, half, 0)
    keep = lax.dynamic_slice_in_dim(product, core * half, half, 0)
    both = keep + lax.ppermute(give, "core", swap)
    parts = lax.all_to_all(both, GRID, 0, 0, tiled=True).reshape(8, BLK, width)
    rows_global = row * rows_loc + core * half + chip * BLK + jnp.arange(BLK, dtype=jnp.int32)
    diag = (rows_global[:, None] == start + jnp.arange(width, dtype=jnp.int32)[None, :]).astype(jnp.float32)
    keep_rows = (rows_global < order // 2) == (rows_global < split_index[0])
    proj = jnp.where(keep_rows[:, None], 0.5 * (diag + jnp.sum(parts, 0)), jnp.float32(0.0))

    turned = lax.ppermute(proj, ALL, turn_perm())
    f = turn_map()
    table = jnp.array([[[f(xx, yy) for yy in range(4)].index(s) for s in range(4)] for xx in range(4)], jnp.int32)
    a, b = x, zh
    out = jnp.zeros((8 * BLK, width), jnp.float32)

    def place(out, got, sx, szh):
        idx = table[y, sx] * 2 + szh
        return lax.dynamic_update_slice_in_dim(out, got, idx * BLK, 0)

    out = place(out, turned, a, b)
    for d1, d2 in OFFS:
        got = lax.ppermute(turned, ROW, offsets(d1, d2))
        out = place(out, got, (a - d1) % 4, (b - d2) % 2)
    return out


def solution(mesh):
    fine = Mesh(mesh.devices.reshape(SIZES), ALL)
    placed = (P(ROW, ("y", "zl", "core")), P(), P(), P())
    return jax.shard_map(
        per_device, mesh=fine, in_specs=placed, out_specs=P(("y", "zl", "core"), None), check_vma=False
    )
```

```python
import jax
import jax.numpy as jnp
from jax import lax
from jax.experimental import pallas as pl
from jax.experimental.pallas import tpu as pltpu
from jax.sharding import Mesh, PartitionSpec as P

ROW = ("x", "zh")
GRID = ("y", "zl")
COL = ("y", "zl", "core")
ALL = ROW + COL
SIZES = (4, 2, 4, 2, 2)
F32, BF16 = jnp.float32, jnp.bfloat16
BLK = 128
CHUNKS = 2


def split(v):
    hi = v.astype(BF16)
    return hi, (v - hi.astype(F32)).astype(BF16)


def dot3(a, b, dims):
    (ah, al), (bh, bl) = split(a), split(b)

    def one(p, q):
        return lax.dot_general(p, q, (dims, ((), ())), preferred_element_type=F32)

    return one(ah, bh) + (one(ah, bl) + one(al, bh))


def gram_kernel(where, m_ref, c_ref, *rest):
    out = rest[-1]

    @pl.when(pl.program_id(0) == 0)
    def _():
        out[...] = rest[0][...] if len(rest) == 2 else jnp.zeros_like(out)

    out[...] += dot3(m_ref[...], c_ref[...], ((0,), (0,)))


def gram_half(matrix, columns, which, prev=None, deep=512):
    rows, width = columns.shape
    cols = matrix.shape[1]
    steps = rows // deep
    ins = [
        pl.BlockSpec((deep, cols), lambda i, s: (s[0] * steps + i, 0)),
        pl.BlockSpec((deep, width), lambda i, s: (i, 0)),
    ]
    args = [matrix, columns]
    if prev is not None:
        ins.append(pl.BlockSpec((cols, width), lambda i, s: (0, 0)))
        args.append(prev)
    return pl.pallas_call(
        gram_kernel,
        out_shape=jax.ShapeDtypeStruct((cols, width), F32),
        grid_spec=pltpu.PrefetchScalarGridSpec(
            num_scalar_prefetch=1,
            grid=(steps,),
            in_specs=ins,
            out_specs=pl.BlockSpec((cols, width), lambda i, s: (0, 0)),
        ),
    )(jnp.reshape(which, (1,)).astype(jnp.int32), *args)


def product_kernel(m_ref, f_ref, out, fh, fl):
    @pl.when(pl.program_id(0) == 0)
    def _():
        fh[...], fl[...] = split(f_ref[...])

    mh, ml = split(m_ref[...])

    def one(p, q):
        return lax.dot_general(p, q, (((1,), (0,)), ((), ())), preferred_element_type=F32)

    out[...] = one(mh, fh[...]) + (one(mh, fl[...]) + one(ml, fh[...]))


def product(matrix, factor, tall=512):
    rows, deep = matrix.shape
    width = factor.shape[1]
    return pl.pallas_call(
        product_kernel,
        out_shape=jax.ShapeDtypeStruct((rows, width), F32),
        grid=(rows // tall,),
        in_specs=[pl.BlockSpec((tall, deep), lambda i: (i, 0)), pl.BlockSpec((deep, width), lambda i: (0, 0))],
        out_specs=pl.BlockSpec((tall, width), lambda i: (i, 0)),
        scratch_shapes=[pltpu.VMEM((deep, width), BF16)] * 2,
    )(matrix, factor)


def ring(v, axes, by):
    return lax.ppermute(v, axes[0], [(i, (i + by) % 4) for i in range(4)])


def flip(v, axis):
    return lax.ppermute(v, axis, [(0, 1), (1, 0)])


def spread(block, axes):
    n = block.shape[0] // 2
    p, m, z = ring(block, axes, 1), ring(block, axes, -1), flip(block, axes[1])
    pz, m2, mz = ring(z, axes, 1), ring(m, axes, -1), flip(m, axes[1])
    u, w = ring(pz[:n], axes, 1), ring(mz[n:], axes, -1)
    return [
        (0, 0, block), (3, 0, p), (1, 0, m), (0, 1, z), (3, 1, pz), (2, 0, m2), (1, 1, mz),
        (2, 1, jnp.concatenate([u, w], 0)),
    ]


def gather(block, axes, place=None):
    a, b = lax.axis_index(axes[0]), lax.axis_index(axes[1])
    rows, width = block.shape
    out = jnp.zeros((8 * rows, width), F32)
    for da, db, got in spread(block, axes):
        sa, sb = (a + da) % 4, (b + db) % 2
        at = sa * 2 + sb if place is None else place(sa, sb)
        out = lax.dynamic_update_slice_in_dim(out, got, at * rows, 0)
    return out


def scatter_sum(partial, axes):
    a, b = lax.axis_index(axes[0]), lax.axis_index(axes[1])
    rows = partial.shape[0] // 8
    n = rows // 2

    def blk(da, db, lo=0, size=rows):
        at = ((a + da) % 4 * 2 + (b + db) % 2) * rows + lo
        return lax.dynamic_slice_in_dim(partial, at, size, 0)

    u, w = ring(blk(2, 1, 0, n), axes, -1), ring(blk(2, 1, n, n), axes, 1)
    sp = ring(blk(2, 0), axes, 1)
    tm = ring(blk(3, 0), axes, -1)
    sz = flip(jnp.concatenate([blk(1, 1, 0, n), blk(1, 1, n, n) + w], 0), axes[1])
    sm = ring(jnp.concatenate([blk(3, 1, 0, n) + u, blk(3, 1, n, n)], 0), axes, -1)
    tp = ring(blk(1, 0) + sz + sp, axes, 1)
    tz = flip(blk(0, 1) + sm, axes[1])
    return blk(0, 0) + tm + tp + tz


SPREAD_X = {0: 2, 1: 3, 3: 1, 2: 0}


def turn(v):
    perm = []
    for x in range(4):
        for zh in range(2):
            for y in range(4):
                for zl in range(2):
                    for c in range(2):
                        src = (((x * 2 + zh) * 4 + y) * 2 + zl) * 2 + c
                        dst = ((((x + SPREAD_X[(y - x) % 4]) % 4 * 2 + zl) * 4 + x) * 2 + zh) * 2 + c
                        perm.append((src, dst))
    return lax.ppermute(v, ALL, perm)


def per_device(matrix, factor_inverse, panel, split_index):
    rows_loc, cols_loc = matrix.shape
    width = factor_inverse.shape[0]
    x, zh = lax.axis_index("x"), lax.axis_index("zh")
    y, zl, core = lax.axis_index("y"), lax.axis_index("zl"), lax.axis_index("core")
    row, chip = x * 2 + zh, y * 2 + zl
    col = chip * 2 + core
    order = cols_loc * 16
    half = rows_loc // 2
    part = width // CHUNKS
    start = panel[0] * width
    owner = start // cols_loc
    offset = start - owner * cols_loc
    chunks = [slice(i * part, (i + 1) * part) for i in range(CHUNKS)]

    give = lax.dynamic_slice(matrix, ((1 - core) * half, offset), (half, width))
    keep = lax.dynamic_slice(matrix, (core * half, offset), (half, width))
    raw = jnp.where(owner % 2 == core, keep, flip(give, "core"))

    first = col * cols_loc + row * BLK - start
    inside = (first >= 0) & (first < width)
    inv_rows = lax.dynamic_slice_in_dim(factor_inverse, jnp.clip(first, 0, width - BLK), BLK, 1).T
    rows_global = row * rows_loc + core * half + chip * BLK + jnp.arange(BLK, dtype=jnp.int32)
    keep_rows = (rows_global < order // 2) == (rows_global < split_index[0])
    diag = (rows_global[:, None] == start + jnp.arange(width, dtype=jnp.int32)[None, :]).astype(F32)

    def place(sx, szh):
        d = sum(jnp.where((y + g) % 4 == sx, k, 0) for k, g in SPREAD_X.items())
        return (y + d) % 4 * 2 + szh

    def panel_of(s):
        mine = lax.dot_general(
            raw, factor_inverse[s], (((1,), (1,)), ((), ())), precision=lax.Precision.HIGH, preferred_element_type=F32
        )
        parts = lax.all_to_all(mine, GRID, 0, 0, tiled=True)
        return gather(lax.dynamic_slice_in_dim(parts, owner // 2 * BLK, BLK, 0), GRID)

    def factor_of(s, own):
        other = flip(own, "core")
        partial = gram_half(matrix, own, core)
        partial = gram_half(matrix, other, 1 - core, partial)
        gram = scatter_sum(partial, ROW) / order
        return gather(gram + jnp.where(inside, inv_rows[:, s], 0.0), ROW)

    def block_of(s, factor):
        made = product(matrix, factor)
        out = lax.dynamic_slice_in_dim(made, (1 - core) * half, half, 0)
        both = lax.dynamic_slice_in_dim(made, core * half, half, 0) + flip(out, "core")
        total = scatter_sum(both, GRID)
        return jnp.where(keep_rows[:, None], 0.5 * (diag[:, s] + total), F32(0.0))

    owns = [panel_of(s) for s in chunks]
    factors = [factor_of(s, o) for s, o in zip(chunks, owns)]
    blocks = [block_of(s, f) for s, f in zip(chunks, factors)]
    return jnp.concatenate([gather(turn(b), ROW, place) for b in blocks], 1)


def solution(mesh):
    fine = Mesh(mesh.devices.reshape(SIZES), ALL)
    placed = (P(ROW, COL), P(), P(), P())
    return jax.shard_map(per_device, mesh=fine, in_specs=placed, out_specs=P(COL, None), check_vma=False)
```

```python
import functools

import jax
import jax.numpy as jnp
from jax import lax
from jax.experimental import pallas as pl
from jax.experimental.pallas import tpu as pltpu
from jax.sharding import Mesh, PartitionSpec as P


ROW = ("x", "zh")
GRID = ("y", "zl")
COL = ("y", "zl", "core")
ALL = ROW + COL
SIZES = (4, 2, 4, 2, 2)
F32, BF16 = jnp.float32, jnp.bfloat16
BLK = 128
REL = ((2, 1), (2, 0), (3, 0), (1, 1), (3, 1), (1, 0), (0, 1), (0, 0))


def split(v):
    hi = v.astype(BF16)
    return hi, (v - hi.astype(F32)).astype(BF16)


def three(ah, al, bh, bl, dims):
    def one(p, q):
        return lax.dot_general(p, q, (dims, ((), ())), preferred_element_type=F32)

    return one(ah, bh) + (one(ah, bl) + one(al, bh))


def join_split(refs, hi, lo):
    @pl.when(pl.program_id(0) == 0)
    def _():
        for k, ref in enumerate(refs):
            rows = pl.ds(k * BLK, BLK)
            hi[rows, :], lo[rows, :] = split(ref[...])


def gram_kernel(n, has_prev, me, *refs):
    m, c, rest = refs[:n], refs[n : 2 * n], refs[2 * n :]
    out, ch, cl = rest[has_prev:]
    join_split(c, ch, cl)
    mh, ml = split(jnp.concatenate([r[...] for r in m], 0))
    made = three(mh, ml, ch[...], cl[...], ((0,), (0,)))
    out[...] = made + rest[0][...] if has_prev else made


def group_spot(s, axis, d):
    return lax.rem(s[axis] + d[0], 4) * 2 + lax.rem(s[axis + 1] + d[1], 2)


def gram_rows(s, d, side):
    return (s[4] if side == 0 else 1 - s[4]) * 8 + group_spot(s, 2, d)


def gram_part(me, matrix, blocks, dists, prev=None, tile=512):
    n, cols, width = len(blocks), matrix.shape[1], blocks[0].shape[1]
    sides = [(d, side) for d in dists for side in (0, 1)]
    ins = [pl.BlockSpec((BLK, tile), lambda i, s, d=d, e=e: (gram_rows(s, d, e), i)) for d, e in sides]
    ins += [pl.BlockSpec((BLK, width), lambda i, s: (0, 0))] * n
    args = [matrix] * n + list(blocks)
    if prev is not None:
        ins.append(pl.BlockSpec((tile, width), lambda i, s: (i, 0)))
        args.append(prev)
    return pl.pallas_call(
        functools.partial(gram_kernel, n, int(prev is not None)),
        out_shape=jax.ShapeDtypeStruct((cols, width), F32),
        grid_spec=pltpu.PrefetchScalarGridSpec(
            num_scalar_prefetch=1,
            grid=(cols // tile,),
            in_specs=ins,
            out_specs=pl.BlockSpec((tile, width), lambda i, s: (i, 0)),
            scratch_shapes=[pltpu.VMEM((n * BLK, width), BF16)] * 2,
        ),
        cost_estimate=pl.CostEstimate(
            flops=6 * n * BLK * cols * width, transcendentals=0, bytes_accessed=4 * n * BLK * (cols + width)
        ),
    )(me, *args)


def gram_last_kernel(n, me, *refs):
    m, c, prev = refs[:n], refs[n : 2 * n], refs[2 * n]
    outs = refs[2 * n + 1 : 2 * n + 1 + len(REL)]
    acc = refs[-1]
    mh, ml = split(jnp.concatenate([r[...] for r in m], 0))
    ch, cl = split(jnp.concatenate([r[...] for r in c], 0))
    acc[...] = prev[...] + three(mh, ml, ch, cl, ((0,), (0,)))
    for out, d in zip(outs, REL):
        out[...] = acc[pl.ds(pl.multiple_of(group_spot(me, 0, d) * BLK, BLK), BLK), :]


def gram_last(me, matrix, blocks, dists, prev):
    n, cols, width = len(blocks), matrix.shape[1], blocks[0].shape[1]
    sides = [(d, side) for d in dists for side in (0, 1)]
    ins = [pl.BlockSpec((BLK, cols), lambda i, s, d=d, e=e: (gram_rows(s, d, e), 0)) for d, e in sides]
    ins += [pl.BlockSpec((BLK, width), lambda i, s: (0, 0))] * n + [pl.BlockSpec((cols, width), lambda i, s: (0, 0))]
    return pl.pallas_call(
        functools.partial(gram_last_kernel, n),
        out_shape=tuple([jax.ShapeDtypeStruct((BLK, width), F32)] * len(REL)),
        grid_spec=pltpu.PrefetchScalarGridSpec(
            num_scalar_prefetch=1,
            grid=(1,),
            in_specs=ins,
            out_specs=tuple([pl.BlockSpec((BLK, width), lambda i, s: (0, 0))] * len(REL)),
            scratch_shapes=[pltpu.VMEM((cols, width), F32)],
        ),
        cost_estimate=pl.CostEstimate(
            flops=6 * n * BLK * cols * width, transcendentals=0, bytes_accessed=4 * n * BLK * (cols + width)
        ),
    )(me, *([matrix] * n), *blocks, prev)


def product_kernel(n, has_prev, me, *refs):
    m, f, rest = refs[:n], refs[n : 2 * n], refs[2 * n :]
    out, fh, fl = rest[has_prev:]
    join_split(f, fh, fl)
    mh, ml = split(jnp.concatenate([r[...] for r in m], 1))
    made = three(mh, ml, fh[...], fl[...], ((1,), (0,)))
    out[...] = made + rest[0][...] if has_prev else made


def product_part(me, matrix, blocks, dists, prev=None, side=None, tile=512):
    n, width = len(blocks), blocks[0].shape[1]
    rows = matrix.shape[0] if side is None else matrix.shape[0] // 2
    steps = rows // tile

    def base(s):
        return 0 if side is None else (s[4] if side == 0 else 1 - s[4]) * steps

    ins = [pl.BlockSpec((tile, BLK), lambda i, s, d=d: (base(s) + i, group_spot(s, 0, d))) for d in dists]
    ins += [pl.BlockSpec((BLK, width), lambda i, s: (0, 0))] * n
    args = [matrix] * n + list(blocks)
    if prev is not None:
        ins.append(pl.BlockSpec((tile, width), lambda i, s: (base(s) + i, 0)))
        args.append(prev)
    return pl.pallas_call(
        functools.partial(product_kernel, n, int(prev is not None)),
        out_shape=jax.ShapeDtypeStruct((rows, width), F32),
        grid_spec=pltpu.PrefetchScalarGridSpec(
            num_scalar_prefetch=1,
            grid=(steps,),
            in_specs=ins,
            out_specs=pl.BlockSpec((tile, width), lambda i, s: (i, 0)),
            scratch_shapes=[pltpu.VMEM((n * BLK, width), BF16)] * 2,
        ),
        cost_estimate=pl.CostEstimate(
            flops=6 * n * BLK * rows * width, transcendentals=0, bytes_accessed=4 * rows * (n * BLK + width)
        ),
    )(me, *args)


def ring(v, axes, by):
    return lax.ppermute(v, axes[0], [(i, (i + by) % 4) for i in range(4)])


def flip(v, axis):
    return lax.ppermute(v, axis, [(0, 1), (1, 0)])


def at(axes, da, db):
    return (lax.axis_index(axes[0]) + da) % 4 * 2 + (lax.axis_index(axes[1]) + db) % 2


def spread(block, axes):
    n = block.shape[0] // 2
    p, m, z = ring(block, axes, 1), ring(block, axes, -1), flip(block, axes[1])
    pz = ring(z, axes, 1)
    m2 = ring(m, axes, -1)
    mz = flip(m, axes[1])
    u = ring(pz[:n], axes, 1)
    w = ring(mz[n:], axes, -1)
    return [
        ((0, 0), block), ((3, 0), p), ((1, 0), m), ((0, 1), z), ((3, 1), pz), ((2, 0), m2), ((1, 1), mz),
        ((2, 1), jnp.concatenate([u, w], 0)),
    ]


def scatter_sum(blk, axes):
    far = blk(2, 1)
    n = far.shape[0] // 2
    u, w = ring(far[:n], axes, -1), ring(far[n:], axes, 1)
    sp, tm = ring(blk(2, 0), axes, 1), ring(blk(3, 0), axes, -1)
    none = jnp.zeros_like(u)
    sz = flip(blk(1, 1) + jnp.concatenate([none, w], 0), axes[1])
    sm = ring(blk(3, 1) + jnp.concatenate([u, none], 0), axes, -1)
    tp = ring(blk(1, 0) + sz + sp, axes, 1)
    tz = flip(blk(0, 1) + sm, axes[1])
    return blk(0, 0) + tm + tp + tz


SPREAD_X = {0: 2, 1: 3, 3: 1, 2: 0}


def turn(v):
    perm = []
    for x in range(4):
        for zh in range(2):
            for y in range(4):
                for zl in range(2):
                    for c in range(2):
                        src = (((x * 2 + zh) * 4 + y) * 2 + zl) * 2 + c
                        dst = ((((x + SPREAD_X[(y - x) % 4]) % 4 * 2 + zl) * 4 + x) * 2 + zh) * 2 + c
                        perm.append((src, dst))
    return lax.ppermute(v, ALL, perm)


def per_device(matrix, factor_inverse, panel, split_index):
    rows_loc, cols_loc = matrix.shape
    width = factor_inverse.shape[0]
    x, zh = lax.axis_index("x"), lax.axis_index("zh")
    y, zl, core = lax.axis_index("y"), lax.axis_index("zl"), lax.axis_index("core")
    row, chip = x * 2 + zh, y * 2 + zl
    col = chip * 2 + core
    order = cols_loc * 16
    half = rows_loc // 2
    start = panel[0] * width
    owner = start // cols_loc
    offset = start - owner * cols_loc

    first = col * cols_loc + row * BLK - start
    inside = (first >= 0) & (first < width)
    inv_rows = lax.dynamic_slice_in_dim(factor_inverse, jnp.clip(first, 0, width - BLK), BLK, 1).T
    inv_rows = jnp.where(inside, inv_rows, F32(0.0))
    rows_global = row * rows_loc + core * half + chip * BLK + jnp.arange(BLK, dtype=jnp.int32)
    keep_rows = (rows_global < order // 2) == (rows_global < split_index[0])
    diag = (rows_global[:, None] == start + jnp.arange(width, dtype=jnp.int32)[None, :]).astype(F32)

    raw = {}
    for da, db in REL:
        j = at(GRID, da, db)
        got = flip(lax.dynamic_slice(matrix, ((1 - core) * half + j * BLK, offset), (BLK, width)), "core")
        kept = lax.dynamic_slice(matrix, (core * half + j * BLK, offset), (BLK, width))
        raw[da, db] = jnp.where(owner // 2 == chip, jnp.where(owner % 2 == core, kept, got), F32(0.0))
    block = scatter_sum(lambda da, db: raw[da, db], GRID)
    block = lax.dot_general(
        block, factor_inverse, (((1,), (1,)), ((), ())), precision=lax.Precision.HIGHEST, preferred_element_type=F32
    )

    me = jnp.stack([x, zh, y, zl, core]).astype(jnp.int32)
    own = [(d, got, flip(got, "core")) for d, got in spread(block, GRID)]

    def both(part):
        return [v for _, p, q in part for v in (p, q)], [d for d, _, _ in part]

    partial = gram_part(me, matrix, *both(own[:4]))
    partial = gram_part(me, matrix, *both(own[4:7]), partial)
    pieces = gram_last(me, matrix, *both(own[7:]), partial)
    parts = dict(zip(REL, pieces))
    block = scatter_sum(lambda da, db: parts[da, db], ROW) / order + inv_rows

    factor = spread(block, ROW)
    blocks, dists = [got for _, got in factor], [d for d, _ in factor]
    partial = product_part(me, matrix, blocks[:4], dists[:4])
    give = product_part(me, matrix, blocks[4:], dists[4:], partial, 1)
    got = flip(give, "core")
    kept = product_part(me, matrix, blocks[4:], dists[4:], partial, 0)

    def held(da, db):
        j = at(GRID, da, db) * BLK
        return lax.dynamic_slice_in_dim(kept, j, BLK, 0) + lax.dynamic_slice_in_dim(got, j, BLK, 0)

    total = scatter_sum(held, GRID)
    block = jnp.where(keep_rows[:, None], 0.5 * (diag + total), F32(0.0))

    out = jnp.zeros((8 * BLK, width), F32)
    for (da, db), got in spread(turn(block), ROW):
        sx, szh = (x + da) % 4, (zh + db) % 2
        d = sum(jnp.where((y + g) % 4 == sx, k, 0) for k, g in SPREAD_X.items())
        out = lax.dynamic_update_slice_in_dim(out, got, ((y + d) % 4 * 2 + szh) * BLK, 0)
    return out


def solution(mesh):
    fine = Mesh(mesh.devices.reshape(SIZES), ALL)
    placed = (P(ROW, COL), P(), P(), P())

    return jax.shard_map(per_device, mesh=fine, in_specs=placed, out_specs=P(COL, None), check_vma=False)
```

```python
import functools

import jax
import jax.numpy as jnp
from jax import lax
from jax.experimental import pallas as pl
from jax.experimental.pallas import tpu as pltpu
from jax.sharding import Mesh, PartitionSpec as P


ROW = ("x", "zh")
GRID = ("y", "zl")
COL = ("y", "zl", "core")
ALL = ROW + COL
SIZES = (4, 2, 4, 2, 2)
F32, BF16 = jnp.float32, jnp.bfloat16
BLK = 128
REL = ((2, 1), (2, 0), (3, 0), (1, 1), (3, 1), (1, 0), (0, 1), (0, 0))


def split(v):
    hi = v.astype(BF16)
    return hi, (v - hi.astype(F32)).astype(BF16)


def three(ah, al, bh, bl, dims):
    def one(p, q):
        return lax.dot_general(p, q, (dims, ((), ())), preferred_element_type=F32)

    return one(ah, bh) + (one(ah, bl) + one(al, bh))


def group_spot(s, axis, d):
    return lax.rem(s[axis] + d[0], 4) * 2 + lax.rem(s[axis + 1] + d[1], 2)


def join_split(refs, spots, hi, lo):
    @pl.when(pl.program_id(0) == 0)
    def _():
        for ref, spot in zip(refs, spots):
            rows = pl.ds(spot * BLK if isinstance(spot, int) else pl.multiple_of(spot * BLK, BLK), BLK)
            hi[rows, :], lo[rows, :] = split(ref[...])


def gram_kernel(dists, pair, me, *refs):
    n = 2 * len(dists)
    m, c, outs, (ch, cl) = refs[:pair], refs[pair : pair + n], refs[pair + n : -2], refs[-2:]
    spots = [side * 8 + group_spot(me, 2, d) for d in dists for side in (me[4], 1 - me[4])]
    join_split(c, spots, ch, cl)
    mh, ml = split(jnp.concatenate([r[...] for r in m], 1) if pair > 1 else m[0][...])
    made = three(mh, ml, ch[...], cl[...], ((0,), (0,)))
    for k in range(len(outs)):

        @pl.when(pl.program_id(0) == k // pair)
        def _(k=k):
            outs[k][...] = made[k % pair * BLK : (k % pair + 1) * BLK]


def gram(me, matrix, blocks, dists, pair=2):
    rows, width = matrix.shape[0], blocks[0].shape[1]

    def column(i, s, e):
        return sum(jnp.where(i == k // pair, group_spot(s, 0, d), 0) for k, d in enumerate(REL) if k % pair == e)

    ins = [pl.BlockSpec((rows, BLK), lambda i, s, e=e: (0, column(i, s, e))) for e in range(pair)]
    ins += [pl.BlockSpec((BLK, width), lambda i, s: (0, 0))] * len(blocks)
    return pl.pallas_call(
        functools.partial(gram_kernel, dists, pair),
        out_shape=tuple([jax.ShapeDtypeStruct((BLK, width), F32)] * len(REL)),
        grid_spec=pltpu.PrefetchScalarGridSpec(
            num_scalar_prefetch=1,
            grid=(len(REL) // pair,),
            in_specs=ins,
            out_specs=tuple([pl.BlockSpec((BLK, width), lambda i, s: (0, 0))] * len(REL)),
            scratch_shapes=[pltpu.VMEM((rows, width), BF16)] * 2,
        ),
    )(me, *([matrix] * pair), *blocks)


def product_kernel(n, has_prev, me, *refs):
    m, f, rest = refs[:n], refs[n : 2 * n], refs[2 * n :]
    out, fh, fl = rest[has_prev:]
    join_split(f, range(n), fh, fl)
    mh, ml = split(jnp.concatenate([r[...] for r in m], 1))
    made = three(mh, ml, fh[...], fl[...], ((1,), (0,)))
    out[...] = made + rest[0][...] if has_prev else made


def product_part(me, matrix, blocks, dists, prev=None, side=None, tile=512):
    n, width = len(blocks), blocks[0].shape[1]
    rows = matrix.shape[0] if side is None else matrix.shape[0] // 2
    steps = rows // tile

    def base(s):
        return 0 if side is None else (s[4] if side == 0 else 1 - s[4]) * steps

    ins = [pl.BlockSpec((tile, BLK), lambda i, s, d=d: (base(s) + i, group_spot(s, 0, d))) for d in dists]
    ins += [pl.BlockSpec((BLK, width), lambda i, s: (0, 0))] * n
    args = [matrix] * n + list(blocks)
    if prev is not None:
        ins.append(pl.BlockSpec((tile, width), lambda i, s: (base(s) + i, 0)))
        args.append(prev)
    return pl.pallas_call(
        functools.partial(product_kernel, n, int(prev is not None)),
        out_shape=jax.ShapeDtypeStruct((rows, width), F32),
        grid_spec=pltpu.PrefetchScalarGridSpec(
            num_scalar_prefetch=1,
            grid=(steps,),
            in_specs=ins,
            out_specs=pl.BlockSpec((tile, width), lambda i, s: (i, 0)),
            scratch_shapes=[pltpu.VMEM((n * BLK, width), BF16)] * 2,
        ),
        cost_estimate=pl.CostEstimate(
            flops=6 * n * BLK * rows * width, transcendentals=0, bytes_accessed=4 * rows * (n * BLK + width)
        ),
    )(me, *args)


def ring(v, axes, by):
    return lax.ppermute(v, axes[0], [(i, (i + by) % 4) for i in range(4)])


def flip(v, axis):
    return lax.ppermute(v, axis, [(0, 1), (1, 0)])


def at(axes, da, db):
    return (lax.axis_index(axes[0]) + da) % 4 * 2 + (lax.axis_index(axes[1]) + db) % 2


def spread(block, axes):
    n = block.shape[0] // 2
    p, m, z = ring(block, axes, 1), ring(block, axes, -1), flip(block, axes[1])
    pz = ring(z, axes, 1)
    m2 = ring(m, axes, -1)
    mz = flip(m, axes[1])
    u = ring(pz[:n], axes, 1)
    w = ring(mz[n:], axes, -1)
    return [
        ((0, 0), block), ((3, 0), p), ((1, 0), m), ((0, 1), z), ((3, 1), pz), ((2, 0), m2), ((1, 1), mz),
        ((2, 1), jnp.concatenate([u, w], 0)),
    ]


def scatter_sum(blk, axes):
    far = blk(2, 1)
    n = far.shape[0] // 2
    u, w = ring(far[:n], axes, -1), ring(far[n:], axes, 1)
    sp, tm = ring(blk(2, 0), axes, 1), ring(blk(3, 0), axes, -1)
    none = jnp.zeros_like(u)
    sz = flip(blk(1, 1) + jnp.concatenate([none, w], 0), axes[1])
    sm = ring(blk(3, 1) + jnp.concatenate([u, none], 0), axes, -1)
    tp = ring(blk(1, 0) + sz + sp, axes, 1)
    tz = flip(blk(0, 1) + sm, axes[1])
    return blk(0, 0) + tm + tp + tz


SPREAD_X = {0: 2, 1: 3, 3: 1, 2: 0}


def turn(v):
    perm = []
    for x in range(4):
        for zh in range(2):
            for y in range(4):
                for zl in range(2):
                    for c in range(2):
                        src = (((x * 2 + zh) * 4 + y) * 2 + zl) * 2 + c
                        dst = ((((x + SPREAD_X[(y - x) % 4]) % 4 * 2 + zl) * 4 + x) * 2 + zh) * 2 + c
                        perm.append((src, dst))
    return lax.ppermute(v, ALL, perm)


def per_device(matrix, factor_inverse, panel, split_index):
    rows_loc, cols_loc = matrix.shape
    width = factor_inverse.shape[0]
    x, zh = lax.axis_index("x"), lax.axis_index("zh")
    y, zl, core = lax.axis_index("y"), lax.axis_index("zl"), lax.axis_index("core")
    row, chip = x * 2 + zh, y * 2 + zl
    col = chip * 2 + core
    order = cols_loc * 16
    half = rows_loc // 2
    start = panel[0] * width
    owner = start // cols_loc
    offset = start - owner * cols_loc

    first = col * cols_loc + row * BLK - start
    inside = (first >= 0) & (first < width)
    inv_rows = lax.dynamic_slice_in_dim(factor_inverse, jnp.clip(first, 0, width - BLK), BLK, 1).T
    inv_rows = jnp.where(inside, inv_rows, F32(0.0))
    rows_global = row * rows_loc + core * half + chip * BLK + jnp.arange(BLK, dtype=jnp.int32)
    keep_rows = (rows_global < order // 2) == (rows_global < split_index[0])
    diag = (rows_global[:, None] == start + jnp.arange(width, dtype=jnp.int32)[None, :]).astype(F32)

    raw, shift = {}, offset
    for da, db in REL:
        j = at(GRID, da, db)
        give = lax.dynamic_slice(matrix, ((1 - core) * half + j * BLK, shift), (BLK, width))
        if not raw:
            give, shift = lax.optimization_barrier((give, offset))
        got = flip(give, "core")
        kept = lax.dynamic_slice(matrix, (core * half + j * BLK, offset if not raw else shift), (BLK, width))
        raw[da, db] = jnp.where(owner // 2 == chip, jnp.where(owner % 2 == core, kept, got), F32(0.0))
    block = scatter_sum(lambda da, db: raw[da, db], GRID)
    block = lax.dot_general(
        block, factor_inverse, (((1,), (1,)), ((), ())), precision=lax.Precision.HIGH, preferred_element_type=F32
    )

    me = jnp.stack([x, zh, y, zl, core]).astype(jnp.int32)
    own = [(d, got, flip(got, "core")) for d, got in spread(block, GRID)]

    pieces = gram(me, matrix, [v for _, p, q in own for v in (p, q)], [d for d, _, _ in own])
    parts = dict(zip(REL, pieces))
    block = scatter_sum(lambda da, db: parts[da, db], ROW) / order + inv_rows

    factor = spread(block, ROW)
    blocks, dists = [got for _, got in factor], [d for d, _ in factor]
    partial = product_part(me, matrix, blocks[:4], dists[:4])
    give = product_part(me, matrix, blocks[4:], dists[4:], partial, 1)
    got = flip(give, "core")
    kept = product_part(me, matrix, blocks[4:], dists[4:], partial, 0)

    def held(da, db):
        j = at(GRID, da, db) * BLK
        return lax.dynamic_slice_in_dim(kept, j, BLK, 0) + lax.dynamic_slice_in_dim(got, j, BLK, 0)

    total = scatter_sum(held, GRID)
    block = jnp.where(keep_rows[:, None], 0.5 * (diag + total), F32(0.0))

    out = jnp.zeros((8 * BLK, width), F32)
    for (da, db), got in spread(turn(block), ROW):
        sx, szh = (x + da) % 4, (zh + db) % 2
        d = sum(jnp.where((y + g) % 4 == sx, k, 0) for k, g in SPREAD_X.items())
        out = lax.dynamic_update_slice_in_dim(out, got, ((y + d) % 4 * 2 + szh) * BLK, 0)
    return out


def solution(mesh):
    fine = Mesh(mesh.devices.reshape(SIZES), ALL)
    placed = (P(ROW, COL), P(), P(), P())

    return jax.shard_map(per_device, mesh=fine, in_specs=placed, out_specs=P(COL, None), check_vma=False)
```

```python
import functools

import jax
import jax.numpy as jnp
from jax import lax
from jax.experimental import pallas as pl
from jax.experimental.pallas import tpu as pltpu
from jax.sharding import Mesh, PartitionSpec as P


ROW = ("x", "zh")
GRID = ("y", "zl")
COL = ("y", "zl", "core")
ALL = ROW + COL
SIZES = (4, 2, 4, 2, 2)
F32, BF16 = jnp.float32, jnp.bfloat16
BLK = 128
REL = ((2, 1), (2, 0), (3, 0), (1, 1), (3, 1), (1, 0), (0, 1), (0, 0))


def split(v):
    hi = v.astype(BF16)
    return hi, (v - hi.astype(F32)).astype(BF16)


def three(ah, al, bh, bl, dims):
    def one(p, q):
        return lax.dot_general(p, q, (dims, ((), ())), preferred_element_type=F32)

    return one(ah, bh) + (one(ah, bl) + one(al, bh))


def group_spot(s, axis, d):
    return lax.rem(s[axis] + d[0], 4) * 2 + lax.rem(s[axis + 1] + d[1], 2)


def join_split(refs, spots, hi, lo):
    @pl.when(pl.program_id(0) == 0)
    def _():
        for ref, spot in zip(refs, spots):
            rows = pl.ds(spot * BLK if isinstance(spot, int) else pl.multiple_of(spot * BLK, BLK), BLK)
            hi[rows, :], lo[rows, :] = split(ref[...])


def gram_kernel(dists, pair, me, *refs):
    n = 2 * len(dists)
    m, c, outs, (ch, cl) = refs[:pair], refs[pair : pair + n], refs[pair + n : -2], refs[-2:]
    spots = [side * 8 + group_spot(me, 2, d) for d in dists for side in (me[4], 1 - me[4])]
    join_split(c, spots, ch, cl)
    mh, ml = split(jnp.concatenate([r[...] for r in m], 1) if pair > 1 else m[0][...])
    made = three(mh, ml, ch[...], cl[...], ((0,), (0,)))
    for k in range(len(outs)):

        @pl.when(pl.program_id(0) == k // pair)
        def _(k=k):
            outs[k][...] = made[k % pair * BLK : (k % pair + 1) * BLK]


def gram(me, matrix, blocks, dists, pair=2):
    rows, width = matrix.shape[0], blocks[0].shape[1]

    def column(i, s, e):
        return sum(jnp.where(i == k // pair, group_spot(s, 0, d), 0) for k, d in enumerate(REL) if k % pair == e)

    ins = [pl.BlockSpec((rows, BLK), lambda i, s, e=e: (0, column(i, s, e))) for e in range(pair)]
    ins += [pl.BlockSpec((BLK, width), lambda i, s: (0, 0))] * len(blocks)
    return pl.pallas_call(
        functools.partial(gram_kernel, dists, pair),
        out_shape=tuple([jax.ShapeDtypeStruct((BLK, width), F32)] * len(REL)),
        grid_spec=pltpu.PrefetchScalarGridSpec(
            num_scalar_prefetch=1,
            grid=(len(REL) // pair,),
            in_specs=ins,
            out_specs=tuple([pl.BlockSpec((BLK, width), lambda i, s: (0, 0))] * len(REL)),
            scratch_shapes=[pltpu.VMEM((rows, width), BF16)] * 2,
        ),
    )(me, *([matrix] * pair), *blocks)


def product_kernel(n, has_prev, me, *refs):
    m, f, rest = refs[:n], refs[n : 2 * n], refs[2 * n :]
    out, fh, fl = rest[has_prev:]
    join_split(f, range(n), fh, fl)
    mh, ml = split(jnp.concatenate([r[...] for r in m], 1))
    made = three(mh, ml, fh[...], fl[...], ((1,), (0,)))
    out[...] = made + rest[0][...] if has_prev else made


def product_part(me, matrix, blocks, dists, prev=None, side=None, tile=512):
    n, width = len(blocks), blocks[0].shape[1]
    rows = matrix.shape[0] if side is None else matrix.shape[0] // 2
    steps = rows // tile

    def base(s):
        return 0 if side is None else (s[4] if side == 0 else 1 - s[4]) * steps

    ins = [pl.BlockSpec((tile, BLK), lambda i, s, d=d: (base(s) + i, group_spot(s, 0, d))) for d in dists]
    ins += [pl.BlockSpec((BLK, width), lambda i, s: (0, 0))] * n
    args = [matrix] * n + list(blocks)
    if prev is not None:
        ins.append(pl.BlockSpec((tile, width), lambda i, s: (base(s) + i, 0)))
        args.append(prev)
    return pl.pallas_call(
        functools.partial(product_kernel, n, int(prev is not None)),
        out_shape=jax.ShapeDtypeStruct((rows, width), F32),
        grid_spec=pltpu.PrefetchScalarGridSpec(
            num_scalar_prefetch=1,
            grid=(steps,),
            in_specs=ins,
            out_specs=pl.BlockSpec((tile, width), lambda i, s: (i, 0)),
            scratch_shapes=[pltpu.VMEM((n * BLK, width), BF16)] * 2,
        ),
        cost_estimate=pl.CostEstimate(
            flops=6 * n * BLK * rows * width, transcendentals=0, bytes_accessed=4 * rows * (n * BLK + width)
        ),
    )(me, *args)


def ring(v, axes, by):
    return lax.ppermute(v, axes[0], [(i, (i + by) % 4) for i in range(4)])


def flip(v, axis):
    return lax.ppermute(v, axis, [(0, 1), (1, 0)])


def at(axes, da, db):
    return (lax.axis_index(axes[0]) + da) % 4 * 2 + (lax.axis_index(axes[1]) + db) % 2


def spread(block, axes):
    n = block.shape[0] // 2
    p, m, z = ring(block, axes, 1), ring(block, axes, -1), flip(block, axes[1])
    pz = ring(z, axes, 1)
    m2 = ring(m, axes, -1)
    mz = flip(m, axes[1])
    u = ring(pz[:n], axes, 1)
    w = ring(mz[n:], axes, -1)
    return [
        ((0, 0), block), ((3, 0), p), ((1, 0), m), ((0, 1), z), ((3, 1), pz), ((2, 0), m2), ((1, 1), mz),
        ((2, 1), jnp.concatenate([u, w], 0)),
    ]


def scatter_sum(blk, axes):
    far = blk(2, 1)
    n = far.shape[0] // 2
    u, w = ring(far[:n], axes, -1), ring(far[n:], axes, 1)
    held = lax.optimization_barrier({d: blk(*d) for d in REL[1:]})
    sp, tm = ring(held[2, 0], axes, 1), ring(held[3, 0], axes, -1)
    none = jnp.zeros_like(u)
    sz = flip(held[1, 1] + jnp.concatenate([none, w], 0), axes[1])
    sm = ring(held[3, 1] + jnp.concatenate([u, none], 0), axes, -1)
    tp = ring(held[1, 0] + sz + sp, axes, 1)
    tz = flip(held[0, 1] + sm, axes[1])
    return held[0, 0] + tm + tp + tz


SPREAD_X = {0: 2, 1: 3, 3: 1, 2: 0}


def turn(v):
    perm = []
    for x in range(4):
        for zh in range(2):
            for y in range(4):
                for zl in range(2):
                    for c in range(2):
                        src = (((x * 2 + zh) * 4 + y) * 2 + zl) * 2 + c
                        dst = ((((x + SPREAD_X[(y - x) % 4]) % 4 * 2 + zl) * 4 + x) * 2 + zh) * 2 + c
                        perm.append((src, dst))
    return lax.ppermute(v, ALL, perm)


def per_device(matrix, factor_inverse, panel, split_index):
    rows_loc, cols_loc = matrix.shape
    width = factor_inverse.shape[0]
    x, zh = lax.axis_index("x"), lax.axis_index("zh")
    y, zl, core = lax.axis_index("y"), lax.axis_index("zl"), lax.axis_index("core")
    row, chip = x * 2 + zh, y * 2 + zl
    col = chip * 2 + core
    order = cols_loc * 16
    half = rows_loc // 2
    start = panel[0] * width
    owner = start // cols_loc
    offset = start - owner * cols_loc

    first = col * cols_loc + row * BLK - start
    inside = (first >= 0) & (first < width)
    inv_rows = lax.dynamic_slice_in_dim(factor_inverse, jnp.clip(first, 0, width - BLK), BLK, 1).T
    inv_rows = jnp.where(inside, inv_rows, F32(0.0))
    rows_global = row * rows_loc + core * half + chip * BLK + jnp.arange(BLK, dtype=jnp.int32)
    keep_rows = (rows_global < order // 2) == (rows_global < split_index[0])
    diag = (rows_global[:, None] == start + jnp.arange(width, dtype=jnp.int32)[None, :]).astype(F32)

    raw, shift = {}, offset
    for da, db in REL:
        j = at(GRID, da, db)
        give = lax.dynamic_slice(matrix, ((1 - core) * half + j * BLK, shift), (BLK, width))
        if not raw:
            give, shift = lax.optimization_barrier((give, offset))
        got = flip(give, "core")
        kept = lax.dynamic_slice(matrix, (core * half + j * BLK, offset if not raw else shift), (BLK, width))
        raw[da, db] = jnp.where(owner // 2 == chip, jnp.where(owner % 2 == core, kept, got), F32(0.0))
    block = scatter_sum(lambda da, db: raw[da, db], GRID)
    block = lax.dot_general(
        block, factor_inverse, (((1,), (1,)), ((), ())), precision=lax.Precision.HIGH, preferred_element_type=F32
    )

    me = jnp.stack([x, zh, y, zl, core]).astype(jnp.int32)
    own = [(d, got, flip(got, "core")) for d, got in spread(block, GRID)]

    pieces = gram(me, matrix, [v for _, p, q in own for v in (p, q)], [d for d, _, _ in own])
    parts = dict(zip(REL, pieces))
    block = scatter_sum(lambda da, db: parts[da, db], ROW) / order + inv_rows

    factor = spread(block, ROW)
    blocks, dists = [got for _, got in factor], [d for d, _ in factor]
    partial = product_part(me, matrix, blocks[:4], dists[:4])
    give = product_part(me, matrix, blocks[4:], dists[4:], partial, 1)
    got = flip(give, "core")
    kept = product_part(me, matrix, blocks[4:], dists[4:], partial, 0)

    def held(da, db):
        j = at(GRID, da, db) * BLK
        return lax.dynamic_slice_in_dim(kept, j, BLK, 0) + lax.dynamic_slice_in_dim(got, j, BLK, 0)

    total = scatter_sum(held, GRID)
    block = jnp.where(keep_rows[:, None], 0.5 * (diag + total), F32(0.0))

    out = jnp.zeros((8 * BLK, width), F32)
    for (da, db), got in spread(turn(block), ROW):
        sx, szh = (x + da) % 4, (zh + db) % 2
        d = sum(jnp.where((y + g) % 4 == sx, k, 0) for k, g in SPREAD_X.items())
        out = lax.dynamic_update_slice_in_dim(out, got, ((y + d) % 4 * 2 + szh) * BLK, 0)
    return out


def solution(mesh):
    fine = Mesh(mesh.devices.reshape(SIZES), ALL)
    placed = (P(ROW, COL), P(), P(), P())

    return jax.shard_map(per_device, mesh=fine, in_specs=placed, out_specs=P(COL, None), check_vma=False)
```

```python
import functools

import jax
import jax.numpy as jnp
from jax import lax
from jax.experimental import pallas as pl
from jax.experimental.pallas import tpu as pltpu
from jax.sharding import Mesh, PartitionSpec as P


ROW = ("x", "zh")
GRID = ("y", "zl")
COL = ("y", "zl", "core")
ALL = ROW + COL
SIZES = (4, 2, 4, 2, 2)
F32, BF16 = jnp.float32, jnp.bfloat16
BLK = 128
REL = ((2, 1), (2, 0), (3, 0), (1, 1), (3, 1), (1, 0), (0, 1), (0, 0))


def split(v):
    hi = v.astype(BF16)
    return hi, (v - hi.astype(F32)).astype(BF16)


def three(ah, al, bh, bl, dims):
    def one(p, q):
        return lax.dot_general(p, q, (dims, ((), ())), preferred_element_type=F32)

    return one(ah, bh) + (one(ah, bl) + one(al, bh))


def group_spot(s, axis, d):
    return lax.rem(s[axis] + d[0], 4) * 2 + lax.rem(s[axis + 1] + d[1], 2)


def join_split(refs, spots, hi, lo):
    @pl.when(pl.program_id(0) == 0)
    def _():
        for ref, spot in zip(refs, spots):
            rows = pl.ds(spot * BLK if isinstance(spot, int) else pl.multiple_of(spot * BLK, BLK), BLK)
            hi[rows, :], lo[rows, :] = split(ref[...])


def gram_kernel(dists, pair, me, *refs):
    n = 2 * len(dists)
    m, c, outs, (ch, cl) = refs[:pair], refs[pair : pair + n], refs[pair + n : -2], refs[-2:]
    spots = [side * 8 + group_spot(me, 2, d) for d in dists for side in (me[4], 1 - me[4])]
    join_split(c, spots, ch, cl)
    mh, ml = split(jnp.concatenate([r[...] for r in m], 1) if pair > 1 else m[0][...])
    made = three(mh, ml, ch[...], cl[...], ((0,), (0,)))
    for k in range(len(outs)):

        @pl.when(pl.program_id(0) == k // pair)
        def _(k=k):
            outs[k][...] = made[k % pair * BLK : (k % pair + 1) * BLK]


def gram(me, matrix, blocks, dists, pair=2):
    rows, width = matrix.shape[0], blocks[0].shape[1]

    def column(i, s, e):
        return sum(jnp.where(i == k // pair, group_spot(s, 0, d), 0) for k, d in enumerate(REL) if k % pair == e)

    ins = [pl.BlockSpec((rows, BLK), lambda i, s, e=e: (0, column(i, s, e))) for e in range(pair)]
    ins += [pl.BlockSpec((BLK, width), lambda i, s: (0, 0))] * len(blocks)
    return pl.pallas_call(
        functools.partial(gram_kernel, dists, pair),
        out_shape=tuple([jax.ShapeDtypeStruct((BLK, width), F32)] * len(REL)),
        grid_spec=pltpu.PrefetchScalarGridSpec(
            num_scalar_prefetch=1,
            grid=(len(REL) // pair,),
            in_specs=ins,
            out_specs=tuple([pl.BlockSpec((BLK, width), lambda i, s: (0, 0))] * len(REL)),
            scratch_shapes=[pltpu.VMEM((rows, width), BF16)] * 2,
        ),
    )(me, *([matrix] * pair), *blocks)


def product_kernel(n, has_prev, me, *refs):
    m, f, rest = refs[:n], refs[n : 2 * n], refs[2 * n :]
    out, fh, fl = rest[has_prev:]
    join_split(f, range(n), fh, fl)
    mh, ml = split(jnp.concatenate([r[...] for r in m], 1))
    made = three(mh, ml, fh[...], fl[...], ((1,), (0,)))
    out[...] = made + rest[0][...] if has_prev else made


def product_part(me, matrix, blocks, dists, prev=None, side=None, tile=512):
    n, width = len(blocks), blocks[0].shape[1]
    rows = matrix.shape[0] if side is None else matrix.shape[0] // 2
    steps = rows // tile

    def base(s):
        return 0 if side is None else (s[4] if side == 0 else 1 - s[4]) * steps

    ins = [pl.BlockSpec((tile, BLK), lambda i, s, d=d: (base(s) + i, group_spot(s, 0, d))) for d in dists]
    ins += [pl.BlockSpec((BLK, width), lambda i, s: (0, 0))] * n
    args = [matrix] * n + list(blocks)
    if prev is not None:
        ins.append(pl.BlockSpec((tile, width), lambda i, s: (base(s) + i, 0)))
        args.append(prev)
    return pl.pallas_call(
        functools.partial(product_kernel, n, int(prev is not None)),
        out_shape=jax.ShapeDtypeStruct((rows, width), F32),
        grid_spec=pltpu.PrefetchScalarGridSpec(
            num_scalar_prefetch=1,
            grid=(steps,),
            in_specs=ins,
            out_specs=pl.BlockSpec((tile, width), lambda i, s: (i, 0)),
            scratch_shapes=[pltpu.VMEM((n * BLK, width), BF16)] * 2,
        ),
        cost_estimate=pl.CostEstimate(
            flops=6 * n * BLK * rows * width, transcendentals=0, bytes_accessed=4 * rows * (n * BLK + width)
        ),
    )(me, *args)


def ring(v, axes, by):
    return lax.ppermute(v, axes[0], [(i, (i + by) % 4) for i in range(4)])


def flip(v, axis):
    return lax.ppermute(v, axis, [(0, 1), (1, 0)])


def at(axes, da, db):
    return (lax.axis_index(axes[0]) + da) % 4 * 2 + (lax.axis_index(axes[1]) + db) % 2


def spread(block, axes):
    n = block.shape[0] // 2
    p, m, z = ring(block, axes, 1), ring(block, axes, -1), flip(block, axes[1])
    pz = ring(z, axes, 1)
    m2 = ring(m, axes, -1)
    mz = flip(m, axes[1])
    u = ring(pz[:n], axes, 1)
    w = ring(mz[n:], axes, -1)
    return [
        ((0, 0), block), ((3, 0), p), ((1, 0), m), ((0, 1), z), ((3, 1), pz), ((2, 0), m2), ((1, 1), mz),
        ((2, 1), jnp.concatenate([u, w], 0)),
    ]


def scatter_sum(blk, axes):
    far = blk(2, 1)
    n = far.shape[0] // 2
    u = ring(far[:n], axes, -1)
    w = ring(far[n:], axes, 1)
    held = lax.optimization_barrier({d: blk(*d) for d in REL[1:]})
    sp, tm = ring(held[2, 0], axes, 1), ring(held[3, 0], axes, -1)
    none = jnp.zeros_like(u)
    sz = flip(held[1, 1] + jnp.concatenate([none, w], 0), axes[1])
    sm = ring(held[3, 1] + jnp.concatenate([u, none], 0), axes, -1)
    tp = ring(held[1, 0] + sz + sp, axes, 1)
    tz = flip(held[0, 1] + sm, axes[1])
    return held[0, 0] + tm + tp + tz


SPREAD_X = {0: 2, 1: 3, 3: 1, 2: 0}


def turn(v):
    perm = []
    for x in range(4):
        for zh in range(2):
            for y in range(4):
                for zl in range(2):
                    for c in range(2):
                        src = (((x * 2 + zh) * 4 + y) * 2 + zl) * 2 + c
                        dst = ((((x + SPREAD_X[(y - x) % 4]) % 4 * 2 + zl) * 4 + x) * 2 + zh) * 2 + c
                        perm.append((src, dst))
    return lax.ppermute(v, ALL, perm)


def per_device(matrix, factor_inverse, panel, split_index):
    rows_loc, cols_loc = matrix.shape
    width = factor_inverse.shape[0]
    x, zh = lax.axis_index("x"), lax.axis_index("zh")
    y, zl, core = lax.axis_index("y"), lax.axis_index("zl"), lax.axis_index("core")
    row, chip = x * 2 + zh, y * 2 + zl
    col = chip * 2 + core
    order = cols_loc * 16
    half = rows_loc // 2
    start = panel[0] * width
    owner = start // cols_loc
    offset = start - owner * cols_loc

    first = col * cols_loc + row * BLK - start
    inside = (first >= 0) & (first < width)
    inv_rows = lax.dynamic_slice_in_dim(factor_inverse, jnp.clip(first, 0, width - BLK), BLK, 1).T
    inv_rows = jnp.where(inside, inv_rows, F32(0.0))
    rows_global = row * rows_loc + core * half + chip * BLK + jnp.arange(BLK, dtype=jnp.int32)
    keep_rows = (rows_global < order // 2) == (rows_global < split_index[0])
    diag = (rows_global[:, None] == start + jnp.arange(width, dtype=jnp.int32)[None, :]).astype(F32)

    raw, shift = {}, offset
    for da, db in REL:
        j = at(GRID, da, db)
        give = lax.dynamic_slice(matrix, ((1 - core) * half + j * BLK, shift), (BLK, width))
        if not raw:
            give, shift = lax.optimization_barrier((give, offset))
        got = flip(give, "core")
        kept = lax.dynamic_slice(matrix, (core * half + j * BLK, offset if not raw else shift), (BLK, width))
        raw[da, db] = jnp.where(owner // 2 == chip, jnp.where(owner % 2 == core, kept, got), F32(0.0))
    block = scatter_sum(lambda da, db: raw[da, db], GRID)
    block = lax.dot_general(
        block, factor_inverse, (((1,), (1,)), ((), ())), precision=lax.Precision.HIGH, preferred_element_type=F32
    )

    me = jnp.stack([x, zh, y, zl, core]).astype(jnp.int32)
    own = [(d, got, flip(got, "core")) for d, got in spread(block, GRID)]

    pieces = gram(me, matrix, [v for _, p, q in own for v in (p, q)], [d for d, _, _ in own])
    parts = dict(zip(REL, pieces))
    block = scatter_sum(lambda da, db: parts[da, db], ROW) / order + inv_rows

    factor = spread(block, ROW)
    blocks, dists = [got for _, got in factor], [d for d, _ in factor]
    partial = product_part(me, matrix, blocks[:4], dists[:4])
    give = product_part(me, matrix, blocks[4:], dists[4:], partial, 1)
    got = flip(give, "core")
    kept = product_part(me, matrix, blocks[4:], dists[4:], partial, 0)

    ready = [kept, got]

    def held(da, db):
        j = at(GRID, da, db) * BLK
        made = lax.dynamic_slice_in_dim(ready[0], j, BLK, 0) + lax.dynamic_slice_in_dim(ready[1], j, BLK, 0)
        if (da, db) == REL[0]:
            made, *ready[:] = lax.optimization_barrier((made, *ready))
        return made

    total = scatter_sum(held, GRID)
    block = jnp.where(keep_rows[:, None], 0.5 * (diag + total), F32(0.0))

    out = jnp.zeros((8 * BLK, width), F32)
    for (da, db), got in spread(turn(block), ROW):
        sx, szh = (x + da) % 4, (zh + db) % 2
        d = sum(jnp.where((y + g) % 4 == sx, k, 0) for k, g in SPREAD_X.items())
        out = lax.dynamic_update_slice_in_dim(out, got, ((y + d) % 4 * 2 + szh) * BLK, 0)
    return out


def solution(mesh):
    fine = Mesh(mesh.devices.reshape(SIZES), ALL)
    placed = (P(ROW, COL), P(), P(), P())

    return jax.shard_map(per_device, mesh=fine, in_specs=placed, out_specs=P(COL, None), check_vma=False)
```

```python
import functools

import jax
import jax.numpy as jnp
from jax import lax
from jax.experimental import pallas as pl
from jax.experimental.pallas import tpu as pltpu
from jax.sharding import Mesh, PartitionSpec as P


ROW = ("x", "zh")
GRID = ("y", "zl")
COL = ("y", "zl", "core")
ALL = ROW + COL
SIZES = (4, 2, 4, 2, 2)
F32, BF16 = jnp.float32, jnp.bfloat16
BLK = 128
REL = ((2, 1), (2, 0), (3, 0), (1, 1), (3, 1), (1, 0), (0, 1), (0, 0))


def split(v):
    hi = v.astype(BF16)
    return hi, (v - hi.astype(F32)).astype(BF16)


def three(ah, al, bh, bl, dims):
    def one(p, q):
        return lax.dot_general(p, q, (dims, ((), ())), preferred_element_type=F32)

    return one(ah, bh) + (one(ah, bl) + one(al, bh))


def group_spot(s, axis, d):
    return lax.rem(s[axis] + d[0], 4) * 2 + lax.rem(s[axis + 1] + d[1], 2)


def join_split(refs, spots, hi, lo):
    @pl.when(pl.program_id(0) == 0)
    def _():
        for ref, spot in zip(refs, spots):
            rows = pl.ds(spot * BLK if isinstance(spot, int) else pl.multiple_of(spot * BLK, BLK), BLK)
            hi[rows, :], lo[rows, :] = split(ref[...])


def gram_kernel(dists, pair, me, *refs):
    n = 2 * len(dists)
    m, c, outs, (ch, cl) = refs[:pair], refs[pair : pair + n], refs[pair + n : -2], refs[-2:]
    spots = [side * 8 + group_spot(me, 2, d) for d in dists for side in (me[4], 1 - me[4])]
    join_split(c, spots, ch, cl)
    mh, ml = split(jnp.concatenate([r[...] for r in m], 1) if pair > 1 else m[0][...])
    made = three(mh, ml, ch[...], cl[...], ((0,), (0,)))
    for k in range(len(outs)):

        @pl.when(pl.program_id(0) == k // pair)
        def _(k=k):
            outs[k][...] = made[k % pair * BLK : (k % pair + 1) * BLK]


def gram(me, matrix, blocks, dists, pair=2):
    rows, width = matrix.shape[0], blocks[0].shape[1]

    def column(i, s, e):
        return sum(jnp.where(i == k // pair, group_spot(s, 0, d), 0) for k, d in enumerate(REL) if k % pair == e)

    ins = [pl.BlockSpec((rows, BLK), lambda i, s, e=e: (0, column(i, s, e))) for e in range(pair)]
    ins += [pl.BlockSpec((BLK, width), lambda i, s: (0, 0))] * len(blocks)
    return pl.pallas_call(
        functools.partial(gram_kernel, dists, pair),
        out_shape=tuple([jax.ShapeDtypeStruct((BLK, width), F32)] * len(REL)),
        grid_spec=pltpu.PrefetchScalarGridSpec(
            num_scalar_prefetch=1,
            grid=(len(REL) // pair,),
            in_specs=ins,
            out_specs=tuple([pl.BlockSpec((BLK, width), lambda i, s: (0, 0))] * len(REL)),
            scratch_shapes=[pltpu.VMEM((rows, width), BF16)] * 2,
        ),
    )(me, *([matrix] * pair), *blocks)


def product_kernel(n, has_prev, me, *refs):
    m, f, rest = refs[:n], refs[n : 2 * n], refs[2 * n :]
    out, fh, fl = rest[has_prev:]
    join_split(f, range(n), fh, fl)
    mh, ml = split(jnp.concatenate([r[...] for r in m], 1))
    made = three(mh, ml, fh[...], fl[...], ((1,), (0,)))
    out[...] = made + rest[0][...] if has_prev else made


def product_part(me, matrix, blocks, dists, prev=None, side=None, tile=512):
    n, width = len(blocks), blocks[0].shape[1]
    rows = matrix.shape[0] if side is None else matrix.shape[0] // 2
    steps = rows // tile

    def base(s):
        return 0 if side is None else (s[4] if side == 0 else 1 - s[4]) * steps

    ins = [pl.BlockSpec((tile, BLK), lambda i, s, d=d: (base(s) + i, group_spot(s, 0, d))) for d in dists]
    ins += [pl.BlockSpec((BLK, width), lambda i, s: (0, 0))] * n
    args = [matrix] * n + list(blocks)
    if prev is not None:
        ins.append(pl.BlockSpec((tile, width), lambda i, s: (base(s) + i, 0)))
        args.append(prev)
    return pl.pallas_call(
        functools.partial(product_kernel, n, int(prev is not None)),
        out_shape=jax.ShapeDtypeStruct((rows, width), F32),
        grid_spec=pltpu.PrefetchScalarGridSpec(
            num_scalar_prefetch=1,
            grid=(steps,),
            in_specs=ins,
            out_specs=pl.BlockSpec((tile, width), lambda i, s: (i, 0)),
            scratch_shapes=[pltpu.VMEM((n * BLK, width), BF16)] * 2,
        ),
        cost_estimate=pl.CostEstimate(
            flops=6 * n * BLK * rows * width, transcendentals=0, bytes_accessed=4 * rows * (n * BLK + width)
        ),
    )(me, *args)


def ring(v, axes, by):
    return lax.ppermute(v, axes[0], [(i, (i + by) % 4) for i in range(4)])


def flip(v, axis):
    return lax.ppermute(v, axis, [(0, 1), (1, 0)])


def at(axes, da, db):
    return (lax.axis_index(axes[0]) + da) % 4 * 2 + (lax.axis_index(axes[1]) + db) % 2


def spread(block, axes):
    n = block.shape[0] // 2
    p, m, z = ring(block, axes, 1), ring(block, axes, -1), flip(block, axes[1])
    pz = ring(z, axes, 1)
    m2 = ring(m, axes, -1)
    mz = flip(m, axes[1])
    u = ring(pz[:n], axes, 1)
    w = ring(mz[n:], axes, -1)
    return [
        ((0, 0), block), ((3, 0), p), ((1, 0), m), ((0, 1), z), ((3, 1), pz), ((2, 0), m2), ((1, 1), mz),
        ((2, 1), jnp.concatenate([u, w], 0)),
    ]


def scatter_sum(blk, axes):
    far = blk(2, 1)
    n = far.shape[0] // 2
    u = ring(far[:n], axes, -1)
    w = ring(far[n:], axes, 1)
    held = lax.optimization_barrier({d: blk(*d) for d in REL[1:]})
    sp, tm = ring(held[2, 0], axes, 1), ring(held[3, 0], axes, -1)
    none = jnp.zeros_like(u)
    sz = flip(held[1, 1] + jnp.concatenate([none, w], 0), axes[1])
    sm = ring(held[3, 1] + jnp.concatenate([u, none], 0), axes, -1)
    tp = ring(held[1, 0] + sz + sp, axes, 1)
    tz = flip(held[0, 1] + sm, axes[1])
    return held[0, 0] + tm + tp + tz


SPREAD_X = {0: 2, 1: 3, 3: 1, 2: 0}


def turn(v):
    perm = []
    for x in range(4):
        for zh in range(2):
            for y in range(4):
                for zl in range(2):
                    for c in range(2):
                        src = (((x * 2 + zh) * 4 + y) * 2 + zl) * 2 + c
                        dst = ((((x + SPREAD_X[(y - x) % 4]) % 4 * 2 + zl) * 4 + x) * 2 + zh) * 2 + c
                        perm.append((src, dst))
    return lax.ppermute(v, ALL, perm)


def per_device(matrix, factor_inverse, panel, split_index):
    rows_loc, cols_loc = matrix.shape
    width = factor_inverse.shape[0]
    x, zh = lax.axis_index("x"), lax.axis_index("zh")
    y, zl, core = lax.axis_index("y"), lax.axis_index("zl"), lax.axis_index("core")
    row, chip = x * 2 + zh, y * 2 + zl
    col = chip * 2 + core
    order = cols_loc * 16
    half = rows_loc // 2
    start = panel[0] * width
    owner = start // cols_loc
    offset = start - owner * cols_loc

    first = col * cols_loc + row * BLK - start
    inside = (first >= 0) & (first < width)
    inv_rows = lax.dynamic_slice_in_dim(factor_inverse, jnp.clip(first, 0, width - BLK), BLK, 1).T
    inv_rows = jnp.where(inside, inv_rows, F32(0.0))
    rows_global = row * rows_loc + core * half + chip * BLK + jnp.arange(BLK, dtype=jnp.int32)
    keep_rows = (rows_global < order // 2) == (rows_global < split_index[0])
    diag = (rows_global[:, None] == start + jnp.arange(width, dtype=jnp.int32)[None, :]).astype(F32)

    raw, shift, later = {}, offset, offset
    for da, db in REL:
        j = at(GRID, da, db)
        give = lax.dynamic_slice(matrix, ((1 - core) * half + j * BLK, shift), (BLK, width))
        if not raw:
            give, shift = lax.optimization_barrier((give, offset))
        got = flip(give, "core")
        kept = lax.dynamic_slice(matrix, (core * half + j * BLK, later), (BLK, width))
        raw[da, db] = jnp.where(owner // 2 == chip, jnp.where(owner % 2 == core, kept, got), F32(0.0))
        if (da, db) == REL[0]:
            raw[da, db], later = lax.optimization_barrier((raw[da, db], offset))
    block = scatter_sum(lambda da, db: raw[da, db], GRID)
    block = lax.dot_general(
        block, factor_inverse, (((1,), (1,)), ((), ())), precision=lax.Precision.HIGH, preferred_element_type=F32
    )

    me = jnp.stack([x, zh, y, zl, core]).astype(jnp.int32)
    own = [(d, got, flip(got, "core")) for d, got in spread(block, GRID)]

    pieces = gram(me, matrix, [v for _, p, q in own for v in (p, q)], [d for d, _, _ in own])
    parts = dict(zip(REL, pieces))
    block = scatter_sum(lambda da, db: parts[da, db], ROW) / order + inv_rows

    factor = spread(block, ROW)
    blocks, dists = [got for _, got in factor], [d for d, _ in factor]
    partial = product_part(me, matrix, blocks[:4], dists[:4])
    give = product_part(me, matrix, blocks[4:], dists[4:], partial, 1)
    got = flip(give, "core")
    kept = product_part(me, matrix, blocks[4:], dists[4:], partial, 0)

    ready = [kept, got]

    def held(da, db):
        j = at(GRID, da, db) * BLK
        made = lax.dynamic_slice_in_dim(ready[0], j, BLK, 0) + lax.dynamic_slice_in_dim(ready[1], j, BLK, 0)
        if (da, db) == REL[0]:
            made, *ready[:] = lax.optimization_barrier((made, *ready))
        return made

    total = scatter_sum(held, GRID)
    block = jnp.where(keep_rows[:, None], 0.5 * (diag + total), F32(0.0))

    out = jnp.zeros((8 * BLK, width), F32)
    for (da, db), got in spread(turn(block), ROW):
        sx, szh = (x + da) % 4, (zh + db) % 2
        d = sum(jnp.where((y + g) % 4 == sx, k, 0) for k, g in SPREAD_X.items())
        out = lax.dynamic_update_slice_in_dim(out, got, ((y + d) % 4 * 2 + szh) * BLK, 0)
    return out


def solution(mesh):
    fine = Mesh(mesh.devices.reshape(SIZES), ALL)
    placed = (P(ROW, COL), P(), P(), P())

    return jax.shard_map(per_device, mesh=fine, in_specs=placed, out_specs=P(COL, None), check_vma=False)
```
